256 devices in a mesh: seq: 64 (over y_lo, x, z), batch: 4 (over y_hi, core).
Axes of the slice: x: 4, y: 4 (y_hi: 2, y_lo: 2; y = y_hi * 2 + y_lo), z: 8, core: 2. Of those that a mesh axis runs over, the one named last changes fastest.
Arguments:
- signal: bfloat16 [524288, 512], P(('batch', 'seq')), parts along dimension 0, may hold values from -6 to 6
- kernel_weight_stack: bfloat16 [2, 1024, 1024], P(None, 'seq'), may hold values from -0.1875 to 0.1875
- blend_weight_stack: bfloat16 [2, 512, 512], P(None, 'seq'), may hold values from -0.25 to 0.25
Outputs:
- layer_outs: bfloat16 [2, 524288, 512], P(None, ('batch', 'seq')), parts along dimension 1
The draws below stay inside these ranges and needn't reach their ends.
There are 4 independent parts, one for each index of `batch`. The reference program is written for one: setup_inputs(seed, part) draws one part's arguments, and reference() takes and returns one part's arrays. A program takes and returns all parts, laid end to end along the dimension named above; an argument that names none is the same for every part. Nothing has to cross between parts.
All inputs are finite; a program needn't handle non-finite values.
Results may differ from the reference program's by a relative error of at most 0.0043.
Values may be sent and summed in bfloat16 or wider, within the bound.
No kernel may reach another device: no remote copies, remote signals or barrier semaphores. Data moves between devices by JAX's collectives and lax.ppermute only.
A program may use at most 64 MiB of HBM per device.

```python
import jax
import jax.numpy as jnp

C = 512
LAYERS = 2
FIRST_SPACING = 1024
LENGTH = 131072


def levels(own_key, shape, pieces, smallest, largest):
    factor_of = 1.0
    for axis_at, parts in pieces:
        heights = jax.random.uniform(jax.random.fold_in(jax.random.fold_in(own_key, 6), axis_at), (parts,), jnp.float32, smallest / len(pieces), largest / len(pieces))
        factor_of = factor_of * jnp.repeat(jnp.exp(heights), shape[axis_at] // parts).reshape((-1,) + (1,) * (len(shape) - 1 - axis_at))
    return factor_of


def normal_values(own_key, shape, spread, reach, pieces=(), dtype=jnp.bfloat16):
    array = spread * jax.random.normal(own_key, shape, jnp.float32)
    if pieces:
        array = array * levels(own_key, shape, pieces, -0.22, 0.18)
    return jnp.clip(array, -reach, reach).astype(dtype)


def setup_inputs(seed: int = 0, part: int = 0) -> dict:
    seeds = jax.random.split(jax.random.key(seed), 4)
    own_keys = jax.random.split(jax.random.fold_in(seeds[3], part), 4)
    return {
        "signal": normal_values(own_keys[0], (LENGTH, C), 1.0, 6.0, ((0, 64),)),
        "kernel_weight_stack": normal_values(seeds[1], (LAYERS, 2 * C, 2 * C), (2 * C) ** -0.5, 0.1875, ((1, 64),)),
        "blend_weight_stack": normal_values(seeds[2], (LAYERS, C, C), C ** -0.5, 0.25, ((1, 64),)),
    }


def reference(signal, kernel_weight_stack, blend_weight_stack):
    hidden = signal
    layer_outs = []
    for layer_position_index in range(LAYERS):
        layer_spacing = FIRST_SPACING * (2 ** layer_position_index)
        if layer_spacing < LENGTH:
            delayed = jnp.concatenate([jnp.zeros((layer_spacing, C), jnp.bfloat16), hidden[:LENGTH - layer_spacing]], axis=0)
        else:
            delayed = jnp.zeros_like(hidden)
        stacked_in = jnp.concatenate([delayed, hidden], axis=1)
        preact = jnp.dot(stacked_in, kernel_weight_stack[layer_position_index], preferred_element_type=jnp.float32)
        gated_output = (jnp.tanh(preact[:, :C]) * jax.nn.sigmoid(preact[:, C:])).astype(jnp.bfloat16)
        mix_out = jnp.dot(gated_output, blend_weight_stack[layer_position_index], preferred_element_type=jnp.float32)
        hidden = (hidden.astype(jnp.float32) + mix_out).astype(jnp.bfloat16)
        layer_outs.append(hidden)
    return jnp.stack(layer_outs)
```

```python
import functools

import jax
import jax.numpy as jnp
from jax import lax
from jax.experimental import pallas as pl
from jax.experimental.pallas import tpu as pltpu
from jax.sharding import PartitionSpec as P


AXES = ("seq", "batch")
YLO, X, Z, YHI, CORE = 2, 4, 8, 2, 2
C = 512
BF, F32 = jnp.bfloat16, jnp.float32
VMEM = pl.BlockSpec(memory_space=pltpu.VMEM)
SMEM = pl.BlockSpec(memory_space=pltpu.SMEM)
ANY = pl.BlockSpec(memory_space=pl.ANY)


def place(ylo, x, z, yhi, core):
    return (((ylo * X + x) * Z + z) * YHI + yhi) * CORE + core


def route(kind, step):
    pairs = []
    for ylo in range(YLO):
        for x in range(X):
            for z in range(Z):
                for yhi in range(YHI):
                    for core in range(CORE):
                        to = [ylo, x, z, yhi, core]
                        if kind == "seq":
                            s = (ylo * X + x) * Z + z + step
                            if s >= YLO * X * Z:
                                continue
                            to[:3] = [s // (X * Z), s // Z % X, s % Z]
                        elif kind == "y":
                            y = (yhi * YLO + ylo + step) % (YHI * YLO)
                            to[0], to[3] = y % YLO, y // YLO
                        elif kind == "x":
                            to[1] = (x + step) % X
                        elif kind == "z":
                            to[2] = (z + step) % Z
                        else:
                            to[4] = 1 - core
                        pairs.append((place(ylo, x, z, yhi, core), place(*to)))
    return pairs


def move(block, kind, step=1):
    return lax.ppermute(block, AXES, route(kind, step))


def params(mib):
    return pltpu.CompilerParams(vmem_limit_bytes=mib << 20)


def pack_kernel(at_ref, k_ref, m_ref, o_ref):
    first = at_ref[3] == 0
    for layer in range(k_ref.shape[0]):
        k = k_ref[layer]
        o_ref[layer, :, :C] = jnp.where(first, k[:, :C], k[:, C:])
        m = m_ref[layer].astype(F32)
        m = jnp.where(first, m[:, :256], m[:, 256:])
        o_ref[layer, :, C:] = jnp.concatenate([m[:, :128], m[:, 128:]], axis=0).astype(BF)


def spread_kernel(at_ref, own_ref, above_ref, below_ref, up_ref, down_ref, o_ref, acc):
    z = at_ref[2]
    sources = [own_ref, above_ref, up_ref.at[0], up_ref.at[1], up_ref.at[2], down_ref.at[0], down_ref.at[1], below_ref]
    for step, source in enumerate(sources):
        to = lax.rem(z + step, Z)
        for layer in range(o_ref.shape[0]):
            o_ref[layer, pl.ds(pl.multiple_of(to * 16, 16), 16), :C] = source[layer, :, :C]
            m = source[layer, :, C:].astype(F32)
            for h in range(2):
                acc[layer, pl.ds(pl.multiple_of(h * 64 + to * 8, 8), 8), :] = m[h * 8 : h * 8 + 8]
    for layer in range(o_ref.shape[0]):
        o_ref[layer, :, C:] = acc[layer].astype(BF)


def build_kernel(at_ref, *refs):
    parts, (w_ref, m_ref, sem) = refs[:16], refs[16:]
    ylo, x, core = at_ref[0], at_ref[1], at_ref[3]
    copies = []
    for i, part in enumerate(parts):
        j, rest = i // 8, i % 8
        c = core if j == 0 else 1 - core
        to = lax.rem(ylo + rest // 4, YLO) * X + lax.rem(x + rest % 4, X)
        rows = pl.ds(pl.multiple_of(to * 128, 128), 128)
        copies.append((part.at[:, :C], w_ref.at[rows, pl.ds(pl.multiple_of(c * C, C), C)]))
        rows = pl.ds(pl.multiple_of(to * 64, 64), 64)
        for h in range(2):
            columns = pl.ds(pl.multiple_of(c * 256 + h * 128, 128), 128)
            copies.append((part.at[h * 64 : h * 64 + 64, C:], m_ref.at[rows, columns]))
    copies = [pltpu.make_async_copy(a, b, sem.at[i]) for i, (a, b) in enumerate(copies)]
    for copy in copies:
        copy.start()
    for copy in copies:
        copy.wait()


TILE = 256


def rows_of(delayed, now, w_ref, m_ref):
    pre = jnp.dot(delayed, w_ref[:C], preferred_element_type=F32) + jnp.dot(now, w_ref[C:], preferred_element_type=F32)
    gate = 0.5 * jnp.tanh(0.5 * pre[:, C:]) + 0.5
    gated = (jnp.tanh(pre[:, :C]) * gate).astype(BF)
    mix = jnp.dot(gated, m_ref[...], preferred_element_type=F32)
    return (now.astype(F32) + mix).astype(BF)


def layer_kernel(d_ref, n_ref, w_ref, m_ref, o_ref):
    @pl.loop(0, d_ref.shape[0] // TILE)
    def _(i):
        rows = pl.ds(pl.multiple_of(i * TILE, TILE), TILE)
        o_ref[rows, :] = rows_of(d_ref[rows, :], n_ref[rows, :], w_ref, m_ref)


def late_kernel(d_ref, n_ref, e_ref, w_ref, m_ref, o_ref, got, sems):
    half = n_ref.shape[0]
    sent = [
        pltpu.make_async_copy(e_ref, o_ref.at[0, :half], sems.at[0]),
        pltpu.make_async_copy(n_ref, o_ref.at[0, half:], sems.at[1]),
    ]
    for copy in sent:
        copy.start()
    for i in range(half // TILE):
        rows = pl.ds(i * TILE, TILE)
        got[rows, :] = rows_of(d_ref[rows, :], n_ref[rows, :], w_ref, m_ref)
        copy = pltpu.make_async_copy(got.at[rows], o_ref.at[1, pl.ds(half + i * TILE, TILE)], sems.at[2 + i])
        copy.start()
        sent.append(copy)
    for copy in sent:
        copy.wait()


def early_kernel(base, d_ref, n_ref, w_ref, m_ref, _, o_ref, got, sems):
    sent = []
    for i in range(d_ref.shape[0] // TILE):
        rows = pl.ds(i * TILE, TILE)
        at = pl.ds(base + i * TILE, TILE)
        got[rows, :] = rows_of(d_ref[rows, :], n_ref[at, :], w_ref, m_ref)
        copy = pltpu.make_async_copy(got.at[rows], o_ref.at[1, at], sems.at[i])
        copy.start()
        sent.append(copy)
    for copy in sent:
        copy.wait()


def cost(rows):
    return pl.CostEstimate(flops=rows * 2 * (4 * C * C + C * C), transcendentals=rows * 2 * C, bytes_accessed=rows * C * 6 + 5 * C * C * 2)


def per_device(signal, kernel_weight_stack, blend_weight_stack):
    layers = kernel_weight_stack.shape[0]
    half = signal.shape[0] // 2
    s, b = lax.axis_index("seq"), lax.axis_index("batch")
    at = jnp.stack([s // (X * Z), s // Z % X, s % Z, b % CORE]).astype(jnp.int32)

    early, late = signal[:half], signal[half:]
    piece = pl.pallas_call(
        pack_kernel,
        out_shape=jax.ShapeDtypeStruct((layers, 16, 640), BF),
        in_specs=[SMEM, VMEM, VMEM],
        out_specs=VMEM,
        compiler_params=params(4),
        name="pack",
    )(at, kernel_weight_stack, blend_weight_stack)

    below = move(piece, "z", 1)
    above = move(piece, "z", -1)
    before_late = move(late, "seq")
    before_early = move(early, "seq")
    three = jnp.stack([below, piece, above])
    up = move(three, "z", -3)
    down = move(three[1:], "z", 3)
    along_z = pl.pallas_call(
        spread_kernel,
        out_shape=jax.ShapeDtypeStruct((layers, 128, 640), BF),
        in_specs=[SMEM] + [VMEM] * 5,
        out_specs=VMEM,
        scratch_shapes=[pltpu.VMEM((layers, 128, 128), F32)],
        compiler_params=params(8),
        name="spread",
    )(at, piece, above, below, up, down)

    weights = []
    for layer in range(layers):
        own = along_z[layer]
        own = [own, move(own, "x", -1), move(own, "x", 2), move(own, "x", 1)]
        own += [move(part, "y", (1, -1)[i % 2]) for i, part in enumerate(own)]
        own += [move(part, "core") for part in own]
        weights.append(
            pl.pallas_call(
                build_kernel,
                out_shape=(jax.ShapeDtypeStruct((2 * C, 2 * C), BF), jax.ShapeDtypeStruct((C, C), BF)),
                in_specs=[SMEM] + [ANY] * 16,
                out_specs=(VMEM, VMEM),
                scratch_shapes=[pltpu.SemaphoreType.DMA((48,))],
                compiler_params=params(8),
                name="build",
            )(at, *own)
        )

    def apply(layer, delayed, now):
        return pl.pallas_call(
            layer_kernel,
            out_shape=jax.ShapeDtypeStruct(now.shape, BF),
            in_specs=[VMEM] * 4,
            out_specs=VMEM,
            compiler_params=params(20),
            cost_estimate=cost(now.shape[0]),
            name="layer",
        )(delayed, now, *weights[layer])

    first_early = apply(0, before_late, early)
    chunk = half // 2
    arriving = [move(first_early[i : i + chunk], "seq") for i in range(0, half, chunk)]
    first_late = apply(0, early, late)
    before_first_late = apply(0, before_early, before_late)
    out_shape = jax.ShapeDtypeStruct((layers, 2 * half, C), BF)
    out = pl.pallas_call(
        late_kernel,
        out_shape=out_shape,
        in_specs=[VMEM] * 5,
        out_specs=ANY,
        scratch_shapes=[pltpu.VMEM((half, C), BF), pltpu.SemaphoreType.DMA((2 + half // TILE,))],
        compiler_params=params(20),
        cost_estimate=cost(half),
        name="late",
    )(before_first_late, first_late, first_early, *weights[1])
    for i, delayed in enumerate(arriving):
        out = pl.pallas_call(
            functools.partial(early_kernel, i * chunk),
            out_shape=out_shape,
            in_specs=[VMEM] * 4 + [ANY],
            out_specs=ANY,
            scratch_shapes=[pltpu.VMEM((chunk, C), BF), pltpu.SemaphoreType.DMA((chunk // TILE,))],
            input_output_aliases={4: 0},
            compiler_params=params(20),
            cost_estimate=cost(chunk),
            name="early",
        )(delayed, first_early, *weights[1], out)
    return out


def solution(mesh):
    return jax.shard_map(
        per_device,
        mesh=mesh,
        in_specs=(P(("batch", "seq"), None), P(None, "seq", None), P(None, "seq", None)),
        out_specs=P(None, ("batch", "seq"), None),
        check_vma=False,
    )
```

```python
import functools

import jax
import jax.numpy as jnp
from jax import lax
from jax.experimental import pallas as pl
from jax.experimental.pallas import tpu as pltpu
from jax.sharding import PartitionSpec as P


AXES = ("seq", "batch")
YLO, X, Z, YHI, CORE = 2, 4, 8, 2, 2
C = 512
BF, F32 = jnp.bfloat16, jnp.float32
VMEM = pl.BlockSpec(memory_space=pltpu.VMEM)
SMEM = pl.BlockSpec(memory_space=pltpu.SMEM)
ANY = pl.BlockSpec(memory_space=pl.ANY)


def place(ylo, x, z, yhi, core):
    return (((ylo * X + x) * Z + z) * YHI + yhi) * CORE + core


def route(kind, step):
    pairs = []
    for ylo in range(YLO):
        for x in range(X):
            for z in range(Z):
                for yhi in range(YHI):
                    for core in range(CORE):
                        to = [ylo, x, z, yhi, core]
                        if kind == "seq":
                            s = (ylo * X + x) * Z + z + step
                            if s >= YLO * X * Z:
                                continue
                            to[:3] = [s // (X * Z), s // Z % X, s % Z]
                        elif kind == "y":
                            y = (yhi * YLO + ylo + (1 if ylo else -1)) % (YHI * YLO)
                            to[0], to[3] = y % YLO, y // YLO
                        elif kind == "x":
                            to[1] = (x + step) % X
                        elif kind == "xz":
                            to[1], to[2] = (x + 1) % X, (z - 1) % Z
                        elif kind == "z":
                            to[2] = (z + step) % Z
                        else:
                            to[4] = 1 - core
                        pairs.append((place(ylo, x, z, yhi, core), place(*to)))
    return pairs


def move(block, kind, step=1):
    return lax.ppermute(block, AXES, route(kind, step))


def params(mib):
    return pltpu.CompilerParams(vmem_limit_bytes=mib << 20)


def pack_kernel(at_ref, k_ref, m_ref, o_ref):
    first = at_ref[3] == 0
    for layer in range(k_ref.shape[0]):
        k = k_ref[layer]
        o_ref[layer, :, :C] = jnp.where(first, k[:, :C], k[:, C:])
        m = m_ref[layer].astype(F32)
        m = jnp.where(first, m[:, :256], m[:, 256:])
        o_ref[layer, :, C:] = jnp.concatenate([m[:, :128], m[:, 128:]], axis=0).astype(BF)


def spread_kernel(at_ref, own_ref, a1_ref, a2_ref, up_ref, down_ref, o_ref, acc):
    z = at_ref[2]
    sources = [own_ref, a1_ref, a2_ref, up_ref.at[0], up_ref.at[1], up_ref.at[2], down_ref.at[0], down_ref.at[1]]
    for step, source in enumerate(sources):
        to = lax.rem(z + step, Z)
        for layer in range(o_ref.shape[0]):
            o_ref[layer, pl.ds(pl.multiple_of(to * 16, 16), 16), :C] = source[layer, :, :C]
            m = source[layer, :, C:].astype(F32)
            for h in range(2):
                acc[layer, pl.ds(pl.multiple_of(h * 64 + to * 8, 8), 8), :] = m[h * 8 : h * 8 + 8]
    for layer in range(o_ref.shape[0]):
        o_ref[layer, :, C:] = acc[layer].astype(BF)


def flat(refs):
    return [part for ref in refs for part in ([ref] if len(ref.shape) == 2 else [ref.at[i] for i in range(ref.shape[0])])]


def join_kernel(*refs):
    for i, part in enumerate(flat(refs[:-1])):
        refs[-1][i] = part[...]


def build_kernel(at_ref, *refs):
    parts, (w_ref, m_ref, sem) = flat(refs[:-3]), refs[-3:]
    ylo, x, core = at_ref[0], at_ref[1], at_ref[3]
    copies = []
    for i, part in enumerate(parts):
        j, rest = i // 8, i % 8
        c = core if j == 0 else 1 - core
        to = lax.rem(ylo + rest % YLO, YLO) * X + lax.rem(x + rest // YLO, X)
        rows = pl.ds(pl.multiple_of(to * 128, 128), 128)
        copies.append((part.at[:, :C], w_ref.at[rows, pl.ds(pl.multiple_of(c * C, C), C)]))
        rows = pl.ds(pl.multiple_of(to * 64, 64), 64)
        for h in range(2):
            columns = pl.ds(pl.multiple_of(c * 256 + h * 128, 128), 128)
            copies.append((part.at[h * 64 : h * 64 + 64, C:], m_ref.at[rows, columns]))
    copies = [pltpu.make_async_copy(a, b, sem.at[i]) for i, (a, b) in enumerate(copies)]
    for copy in copies:
        copy.start()
    for copy in copies:
        copy.wait()


TILE, BLOCK = 512, 256


def rows_of(delayed, now, w_ref, m_ref):
    both = jnp.concatenate([delayed, now], axis=1)
    gated = []
    for at in range(0, C, BLOCK):
        f = jnp.dot(both, w_ref[:, at : at + BLOCK], preferred_element_type=F32)
        g = jnp.dot(both, w_ref[:, C + at : C + at + BLOCK], preferred_element_type=F32)
        gated.append((jnp.tanh(f) * (0.5 * jnp.tanh(0.5 * g) + 0.5)).astype(BF))
    mix = jnp.dot(jnp.concatenate(gated, axis=1), m_ref[...], preferred_element_type=F32)
    return (now.astype(F32) + mix).astype(BF)


def tile_of(rows):
    return next(t for t in (TILE, TILE // 2, TILE // 4) if rows % t == 0)


def layer_kernel(count, base, *refs):
    n_d, n_n = count
    ds, ns, (w_ref, m_ref, o_ref), held = refs[:n_d], refs[n_d : n_d + n_n], refs[n_d + n_n : n_d + n_n + 3], refs[n_d + n_n + 3 :]
    whole = []
    for parts in (ds, ns):
        if len(parts) > 1:
            ref, held = held[0], held[1:]
            at = 0
            for part in parts:
                ref[at : at + part.shape[0], :] = part[...]
                at += part.shape[0]
            parts = [ref]
        whole.append(parts[0])
    d_ref, n_ref = whole

    tile = tile_of(o_ref.shape[0])

    @pl.loop(0, o_ref.shape[0] // tile)
    def _(i):
        at = pl.multiple_of(i * tile, tile)
        rows = pl.ds(at, tile)
        there = pl.ds(base + at, tile)
        o_ref[rows, :] = rows_of(d_ref[there, :], n_ref[there, :], w_ref, m_ref)


def late_kernel(d_ref, n_ref, *refs):
    es, (w_ref, m_ref, o_ref, got, sems) = refs[:-5], refs[-5:]
    half = n_ref.shape[0]
    tiles = half // TILE
    sent = [pltpu.make_async_copy(n_ref, o_ref.at[0, half:], sems.at[tiles])]
    at = 0
    for i, e_ref in enumerate(es):
        sent.append(pltpu.make_async_copy(e_ref, o_ref.at[0, at : at + e_ref.shape[0]], sems.at[tiles + 1 + i]))
        at += e_ref.shape[0]
    for copy in sent:
        copy.start()

    def out(i):
        at = pl.multiple_of(i * TILE, TILE)
        return pltpu.make_async_copy(got.at[pl.ds(at, TILE)], o_ref.at[1, pl.ds(half + at, TILE)], sems.at[i])

    @pl.loop(0, tiles)
    def _(i):
        rows = pl.ds(pl.multiple_of(i * TILE, TILE), TILE)
        got[rows, :] = rows_of(d_ref[rows, :], n_ref[rows, :], w_ref, m_ref)
        out(i).start()

    for i in range(tiles):
        sent.append(out(i))
    for copy in sent:
        copy.wait()


def early_kernel(base, d_ref, n_ref, w_ref, m_ref, _, o_ref, got, sems):
    tile = tile_of(d_ref.shape[0])
    tiles = d_ref.shape[0] // tile

    def out(i):
        at = pl.multiple_of(i * tile, tile)
        return pltpu.make_async_copy(got.at[pl.ds(at, tile)], o_ref.at[1, pl.ds(base + at, tile)], sems.at[i])

    @pl.loop(0, tiles)
    def _(i):
        rows = pl.ds(pl.multiple_of(i * tile, tile), tile)
        got[rows, :] = rows_of(d_ref[rows, :], n_ref[rows, :], w_ref, m_ref)
        out(i).start()

    for i in range(tiles):
        out(i).wait()


def cost(rows):
    return pl.CostEstimate(flops=rows * 2 * (4 * C * C + C * C), transcendentals=rows * 2 * C, bytes_accessed=rows * C * 6 + 5 * C * C * 2)


def per_device(signal, kernel_weight_stack, blend_weight_stack):
    layers = kernel_weight_stack.shape[0]
    half = signal.shape[0] // 2
    s, b = lax.axis_index("seq"), lax.axis_index("batch")
    at = jnp.stack([s // (X * Z), s // Z % X, s % Z, b % CORE]).astype(jnp.int32)

    early, late = signal[:half], signal[half:]
    piece = pl.pallas_call(
        pack_kernel,
        out_shape=jax.ShapeDtypeStruct((layers, 16, 640), BF),
        in_specs=[SMEM, VMEM, VMEM],
        out_specs=VMEM,
        compiler_params=params(4),
        name="pack",
    )(at, kernel_weight_stack, blend_weight_stack)

    pieces = lax.optimization_barrier((late[:384], late[384:]))
    before_late = [move(piece, "seq") for piece in pieces]
    before_early = [move(early, "seq")]
    a1, a2 = move(piece, "z", -1), move(piece, "z", -2)
    down = move(jnp.stack([piece, a1]), "z", 2)
    up = move(jnp.stack([piece, a1, a2]), "z", -3)
    along_z = pl.pallas_call(
        spread_kernel,
        out_shape=jax.ShapeDtypeStruct((layers, 128, 640), BF),
        in_specs=[SMEM] + [VMEM] * 5,
        out_specs=VMEM,
        scratch_shapes=[pltpu.VMEM((layers, 128, 128), F32)],
        compiler_params=params(8),
        name="spread",
    )(at, piece, a1, a2, up, down)

    def join(*parts):
        count = sum(part.size for part in parts) // (128 * 640)
        return pl.pallas_call(
            join_kernel,
            out_shape=jax.ShapeDtypeStruct((count, 128, 640), BF),
            in_specs=[VMEM] * len(parts),
            out_specs=VMEM,
            compiler_params=params(8),
            name="join",
        )(*parts)

    swapped = move(along_z, "y")
    weights = []
    for layer in range(layers):
        own, other = along_z[layer], swapped[layer]
        if layer == 0:
            ahead = move(own, "x", -1)
            along_x = [own, ahead, move(ahead, "x", -1), move(own, "xz")]
            others = [other] + [move(along_x[i], "y") for i in range(1, X)]
            own = [part for pair in zip(along_x, others) for part in pair]
            own += [move(part, "core") for part in own]
        else:
            pairs = [join(own, other)]
            for _ in range(1, X):
                pairs.append(move(pairs[-1], "x", -1))
            own = [join(*pairs)]
            own.append(move(own[0], "core"))
        weights.append(
            pl.pallas_call(
                build_kernel,
                out_shape=(jax.ShapeDtypeStruct((2 * C, 2 * C), BF), jax.ShapeDtypeStruct((C, C), BF)),
                in_specs=[SMEM] + [ANY] * len(own),
                out_specs=(VMEM, VMEM),
                scratch_shapes=[pltpu.SemaphoreType.DMA((48,))],
                compiler_params=params(8),
                name="build",
            )(at, *own)
        )

    def apply(delayed, now, base, rows):
        now = now if isinstance(now, list) else [now]
        held = [pltpu.VMEM((half, C), BF) for parts in (delayed, now) if len(parts) > 1]
        return pl.pallas_call(
            functools.partial(layer_kernel, (len(delayed), len(now)), base),
            out_shape=jax.ShapeDtypeStruct((rows, C), BF),
            in_specs=[VMEM] * (len(delayed) + len(now) + 2),
            out_specs=VMEM,
            scratch_shapes=held,
            compiler_params=params(20),
            cost_estimate=cost(rows),
            name="layer",
        )(*delayed, *now, *weights[0])

    first_early, arriving, base = [], [], 0
    for rows in (half // 4 * 3, half // 4):
        first_early.append(apply(before_late, early, base, rows))
        arriving.append((base, first_early[-1], move(first_early[-1], "seq")))
        base += rows
    first_late = apply([early], late, 0, half)
    before_first_late = apply(before_early, before_late, 0, half)
    out_shape = jax.ShapeDtypeStruct((layers, 2 * half, C), BF)
    out = pl.pallas_call(
        late_kernel,
        out_shape=out_shape,
        in_specs=[VMEM] * (4 + len(first_early)),
        out_specs=ANY,
        scratch_shapes=[pltpu.VMEM((half, C), BF), pltpu.SemaphoreType.DMA((1 + len(first_early) + half // TILE,))],
        compiler_params=params(20),
        cost_estimate=cost(half),
        name="late",
    )(before_first_late, first_late, *first_early, *weights[1])
    for base, now, delayed in arriving:
        rows = delayed.shape[0]
        out = pl.pallas_call(
            functools.partial(early_kernel, base),
            out_shape=out_shape,
            in_specs=[VMEM] * 4 + [ANY],
            out_specs=ANY,
            scratch_shapes=[pltpu.VMEM((rows, C), BF), pltpu.SemaphoreType.DMA((rows // tile_of(rows),))],
            input_output_aliases={4: 0},
            compiler_params=params(20),
            cost_estimate=cost(rows),
            name="early",
        )(delayed, now, *weights[1], out)
    return out


def solution(mesh):
    return jax.shard_map(
        per_device,
        mesh=mesh,
        in_specs=(P(("batch", "seq"), None), P(None, "seq", None), P(None, "seq", None)),
        out_specs=P(None, ("batch", "seq"), None),
        check_vma=False,
    )
```

```python
import functools

import jax
import jax.numpy as jnp
from jax import lax
from jax.experimental import pallas as pl
from jax.experimental.pallas import tpu as pltpu
from jax.sharding import PartitionSpec as P


AXES = ("seq", "batch")
YLO, X, Z, YHI, CORE = 2, 4, 8, 2, 2
C = 512
BF, F32 = jnp.bfloat16, jnp.float32
VMEM = pl.BlockSpec(memory_space=pltpu.VMEM)
SMEM = pl.BlockSpec(memory_space=pltpu.SMEM)
ANY = pl.BlockSpec(memory_space=pl.ANY)


def place(ylo, x, z, yhi, core):
    return (((ylo * X + x) * Z + z) * YHI + yhi) * CORE + core


def route(kind, step):
    pairs = []
    for ylo in range(YLO):
        for x in range(X):
            for z in range(Z):
                for yhi in range(YHI):
                    for core in range(CORE):
                        to = [ylo, x, z, yhi, core]
                        if kind == "seq":
                            s = (ylo * X + x) * Z + z + step
                            if s >= YLO * X * Z:
                                continue
                            to[:3] = [s // (X * Z), s // Z % X, s % Z]
                        elif kind == "y":
                            y = (yhi * YLO + ylo + (1 if ylo else -1)) % (YHI * YLO)
                            to[0], to[3] = y % YLO, y // YLO
                        elif kind == "x":
                            to[1] = (x + step) % X
                        elif kind == "xz":
                            to[1], to[2] = (x + 1) % X, (z - 1) % Z
                        elif kind == "z":
                            to[2] = (z + step) % Z
                        else:
                            to[4] = 1 - core
                        pairs.append((place(ylo, x, z, yhi, core), place(*to)))
    return pairs


def move(block, kind, step=1):
    return lax.ppermute(block, AXES, route(kind, step))


def params(mib):
    return pltpu.CompilerParams(vmem_limit_bytes=mib << 20)


def pack_kernel(at_ref, k_ref, m_ref, o_ref):
    first = at_ref[3] == 0
    for layer in range(k_ref.shape[0]):
        k = k_ref[layer]
        o_ref[layer, :, :C] = jnp.where(first, k[:, :C], k[:, C:])
        m = m_ref[layer].astype(F32)
        m = jnp.where(first, m[:, :256], m[:, 256:])
        o_ref[layer, :, C:] = jnp.concatenate([m[:, :128], m[:, 128:]], axis=0).astype(BF)


def spread_kernel(at_ref, own_ref, a1_ref, a2_ref, up_ref, down_ref, o_ref, acc):
    z = at_ref[2]
    sources = [own_ref, a1_ref, a2_ref, up_ref.at[0], up_ref.at[1], up_ref.at[2], down_ref.at[0], down_ref.at[1]]
    for step, source in enumerate(sources):
        to = lax.rem(z + step, Z)
        for layer in range(o_ref.shape[0]):
            o_ref[layer, pl.ds(pl.multiple_of(to * 16, 16), 16), :C] = source[layer, :, :C]
            m = source[layer, :, C:].astype(F32)
            for h in range(2):
                acc[layer, pl.ds(pl.multiple_of(h * 64 + to * 8, 8), 8), :] = m[h * 8 : h * 8 + 8]
    for layer in range(o_ref.shape[0]):
        o_ref[layer, :, C:] = acc[layer].astype(BF)


def flat(refs):
    return [part for ref in refs for part in ([ref] if len(ref.shape) == 2 else [ref.at[i] for i in range(ref.shape[0])])]


def join_kernel(*refs):
    for i, part in enumerate(flat(refs[:-1])):
        refs[-1][i] = part[...]


def build_kernel(at_ref, *refs):
    parts, (w_ref, m_ref, sem) = flat(refs[:-3]), refs[-3:]
    ylo, x, core = at_ref[0], at_ref[1], at_ref[3]
    copies = []
    for i, part in enumerate(parts):
        j, rest = i // 8, i % 8
        c = core if j == 0 else 1 - core
        to = lax.rem(ylo + rest % YLO, YLO) * X + lax.rem(x + rest // YLO, X)
        rows = pl.ds(pl.multiple_of(to * 128, 128), 128)
        copies.append((part.at[:, :C], w_ref.at[rows, pl.ds(pl.multiple_of(c * C, C), C)]))
        rows = pl.ds(pl.multiple_of(to * 64, 64), 64)
        for h in range(2):
            columns = pl.ds(pl.multiple_of(c * 256 + h * 128, 128), 128)
            copies.append((part.at[h * 64 : h * 64 + 64, C:], m_ref.at[rows, columns]))
    copies = [pltpu.make_async_copy(a, b, sem.at[i]) for i, (a, b) in enumerate(copies)]
    for copy in copies:
        copy.start()
    for copy in copies:
        copy.wait()


TILE, BLOCK = 256, 256


def rows_of(delayed, now, w_ref, m_ref):
    both = jnp.concatenate([delayed, now], axis=1)
    gated = []
    for at in range(0, C, BLOCK):
        f = jnp.dot(both, w_ref[:, at : at + BLOCK], preferred_element_type=F32)
        g = jnp.dot(both, w_ref[:, C + at : C + at + BLOCK], preferred_element_type=F32)
        gated.append((jnp.tanh(f) * (0.5 * jnp.tanh(0.5 * g) + 0.5)).astype(BF))
    mix = jnp.dot(jnp.concatenate(gated, axis=1), m_ref[...], preferred_element_type=F32)
    return (now.astype(F32) + mix).astype(BF)


def layer_kernel(count, base, *refs):
    n_d, n_n = count
    ds, ns, (w_ref, m_ref, o_ref), held = refs[:n_d], refs[n_d : n_d + n_n], refs[n_d + n_n : n_d + n_n + 3], refs[n_d + n_n + 3 :]
    whole = []
    for parts in (ds, ns):
        if len(parts) > 1:
            ref, held = held[0], held[1:]
            at = 0
            for part in parts:
                ref[at : at + part.shape[0], :] = part[...]
                at += part.shape[0]
            parts = [ref]
        whole.append(parts[0])
    d_ref, n_ref = whole

    for at in range(0, o_ref.shape[0], TILE):
        rows, there = pl.ds(at, TILE), pl.ds(base + at, TILE)
        o_ref[rows, :] = rows_of(d_ref[there, :], n_ref[there, :], w_ref, m_ref)


def late_kernel(d_ref, n_ref, *refs):
    es, (w_ref, m_ref, o_ref, got, sems) = refs[:-5], refs[-5:]
    half = n_ref.shape[0]
    tiles = half // TILE
    sent = [pltpu.make_async_copy(n_ref, o_ref.at[0, half:], sems.at[tiles])]
    at = 0
    for i, e_ref in enumerate(es):
        sent.append(pltpu.make_async_copy(e_ref, o_ref.at[0, at : at + e_ref.shape[0]], sems.at[tiles + 1 + i]))
        at += e_ref.shape[0]
    for copy in sent:
        copy.start()

    for i in range(tiles):
        rows = pl.ds(i * TILE, TILE)
        got[rows, :] = rows_of(d_ref[rows, :], n_ref[rows, :], w_ref, m_ref)
        copy = pltpu.make_async_copy(got.at[rows], o_ref.at[1, pl.ds(half + i * TILE, TILE)], sems.at[i])
        copy.start()
        sent.append(copy)
    for copy in sent:
        copy.wait()


def early_kernel(base, d_ref, n_ref, w_ref, m_ref, _, o_ref, got, sems):
    sent = []
    for i in range(d_ref.shape[0] // TILE):
        rows = pl.ds(i * TILE, TILE)
        got[rows, :] = rows_of(d_ref[rows, :], n_ref[rows, :], w_ref, m_ref)
        copy = pltpu.make_async_copy(got.at[rows], o_ref.at[1, pl.ds(base + i * TILE, TILE)], sems.at[i])
        copy.start()
        sent.append(copy)
    for copy in sent:
        copy.wait()


def cost(rows):
    return pl.CostEstimate(flops=rows * 2 * (4 * C * C + C * C), transcendentals=rows * 2 * C, bytes_accessed=rows * C * 6 + 5 * C * C * 2)


def per_device(signal, kernel_weight_stack, blend_weight_stack):
    layers = kernel_weight_stack.shape[0]
    half = signal.shape[0] // 2
    s, b = lax.axis_index("seq"), lax.axis_index("batch")
    at = jnp.stack([s // (X * Z), s // Z % X, s % Z, b % CORE]).astype(jnp.int32)

    early, late = signal[:half], signal[half:]
    piece = pl.pallas_call(
        pack_kernel,
        out_shape=jax.ShapeDtypeStruct((layers, 16, 640), BF),
        in_specs=[SMEM, VMEM, VMEM],
        out_specs=VMEM,
        compiler_params=params(4),
        name="pack",
    )(at, kernel_weight_stack, blend_weight_stack)

    before_late = [move(late[: half // 2], "seq"), move(late[half // 2 :], "seq")]
    before_early = [move(early, "seq")]
    a1, a2 = move(piece, "z", -1), move(piece, "z", -2)
    down = move(jnp.stack([piece, a1]), "z", 2)
    up = move(jnp.stack([piece, a1, a2]), "z", -3)
    along_z = pl.pallas_call(
        spread_kernel,
        out_shape=jax.ShapeDtypeStruct((layers, 128, 640), BF),
        in_specs=[SMEM] + [VMEM] * 5,
        out_specs=VMEM,
        scratch_shapes=[pltpu.VMEM((layers, 128, 128), F32)],
        compiler_params=params(8),
        name="spread",
    )(at, piece, a1, a2, up, down)

    def join(*parts):
        count = sum(part.size for part in parts) // (128 * 640)
        return pl.pallas_call(
            join_kernel,
            out_shape=jax.ShapeDtypeStruct((count, 128, 640), BF),
            in_specs=[VMEM] * len(parts),
            out_specs=VMEM,
            compiler_params=params(8),
            name="join",
        )(*parts)

    swapped = move(along_z, "y")
    weights = []
    for layer in range(layers):
        own, other = along_z[layer], swapped[layer]
        if layer == 0:
            ahead = move(own, "x", -1)
            along_x = [own, ahead, move(ahead, "x", -1), move(own, "xz")]
            others = [other] + [move(along_x[i], "y") for i in range(1, X)]
            own = [part for pair in zip(along_x, others) for part in pair]
            own += [move(part, "core") for part in own]
        else:
            pairs = [join(own, other)]
            for _ in range(1, X):
                pairs.append(move(pairs[-1], "x", -1))
            own = [join(*pairs)]
            own.append(move(own[0], "core"))
        weights.append(
            pl.pallas_call(
                build_kernel,
                out_shape=(jax.ShapeDtypeStruct((2 * C, 2 * C), BF), jax.ShapeDtypeStruct((C, C), BF)),
                in_specs=[SMEM] + [ANY] * len(own),
                out_specs=(VMEM, VMEM),
                scratch_shapes=[pltpu.SemaphoreType.DMA((48,))],
                compiler_params=params(8),
                name="build",
            )(at, *own)
        )

    def apply(delayed, now, base, rows):
        now = now if isinstance(now, list) else [now]
        held = [pltpu.VMEM((half, C), BF) for parts in (delayed, now) if len(parts) > 1]
        return pl.pallas_call(
            functools.partial(layer_kernel, (len(delayed), len(now)), base),
            out_shape=jax.ShapeDtypeStruct((rows, C), BF),
            in_specs=[VMEM] * (len(delayed) + len(now) + 2),
            out_specs=VMEM,
            scratch_shapes=held,
            compiler_params=params(20),
            cost_estimate=cost(rows),
            name="layer",
        )(*delayed, *now, *weights[0])

    first_early, arriving, base = [], [], 0
    for rows in (half // 4 * 3, half // 4):
        first_early.append(apply(before_late, early, base, rows))
        arriving.append((base, first_early[-1], move(first_early[-1], "seq")))
        base += rows
    first_late = apply([early], late, 0, half)
    before_first_late = apply(before_early, before_late, 0, half)
    out_shape = jax.ShapeDtypeStruct((layers, 2 * half, C), BF)
    out = pl.pallas_call(
        late_kernel,
        out_shape=out_shape,
        in_specs=[VMEM] * (4 + len(first_early)),
        out_specs=ANY,
        scratch_shapes=[pltpu.VMEM((half, C), BF), pltpu.SemaphoreType.DMA((1 + len(first_early) + half // TILE,))],
        compiler_params=params(20),
        cost_estimate=cost(half),
        name="late",
    )(before_first_late, first_late, *first_early, *weights[1])
    for base, now, delayed in arriving:
        rows = delayed.shape[0]
        out = pl.pallas_call(
            functools.partial(early_kernel, base),
            out_shape=out_shape,
            in_specs=[VMEM] * 4 + [ANY],
            out_specs=ANY,
            scratch_shapes=[pltpu.VMEM((rows, C), BF), pltpu.SemaphoreType.DMA((rows // TILE,))],
            input_output_aliases={4: 0},
            compiler_params=params(20),
            cost_estimate=cost(rows),
            name="early",
        )(delayed, now, *weights[1], out)
    return out


def solution(mesh):
    return jax.shard_map(
        per_device,
        mesh=mesh,
        in_specs=(P(("batch", "seq"), None), P(None, "seq", None), P(None, "seq", None)),
        out_specs=P(None, ("batch", "seq"), None),
        check_vma=False,
    )
```

```python
import functools

import jax
import jax.numpy as jnp
from jax import lax
from jax.experimental import pallas as pl
from jax.experimental.pallas import tpu as pltpu
from jax.sharding import PartitionSpec as P


AXES = ("seq", "batch")
YLO, X, Z, YHI, CORE = 2, 4, 8, 2, 2
C = 512
BF, F32 = jnp.bfloat16, jnp.float32
VMEM = pl.BlockSpec(memory_space=pltpu.VMEM)
SMEM = pl.BlockSpec(memory_space=pltpu.SMEM)
ANY = pl.BlockSpec(memory_space=pl.ANY)


def place(ylo, x, z, yhi, core):
    return (((ylo * X + x) * Z + z) * YHI + yhi) * CORE + core


def route(kind, step):
    pairs = []
    for ylo in range(YLO):
        for x in range(X):
            for z in range(Z):
                for yhi in range(YHI):
                    for core in range(CORE):
                        to = [ylo, x, z, yhi, core]
                        if kind == "seq":
                            s = (ylo * X + x) * Z + z + step
                            if s >= YLO * X * Z:
                                continue
                            to[:3] = [s // (X * Z), s // Z % X, s % Z]
                        elif kind == "y":
                            y = (yhi * YLO + ylo + (1 if ylo else -1)) % (YHI * YLO)
                            to[0], to[3] = y % YLO, y // YLO
                        elif kind == "x":
                            to[1] = (x + step) % X
                        elif kind == "xz":
                            to[1], to[2] = (x + 1) % X, (z - 1) % Z
                        elif kind == "z":
                            to[2] = (z + step) % Z
                        else:
                            to[4] = 1 - core
                        pairs.append((place(ylo, x, z, yhi, core), place(*to)))
    return pairs


def move(block, kind, step=1):
    return lax.ppermute(block, AXES, route(kind, step))


def params(mib):
    return pltpu.CompilerParams(vmem_limit_bytes=mib << 20)


def pack_kernel(at_ref, k_ref, m_ref, o_ref):
    first = at_ref[3] == 0
    for layer in range(k_ref.shape[0]):
        k = k_ref[layer]
        o_ref[layer, :, :C] = jnp.where(first, k[:, :C], k[:, C:])
        m = m_ref[layer].astype(F32)
        m = jnp.where(first, m[:, :256], m[:, 256:])
        o_ref[layer, :, C:] = jnp.concatenate([m[:, :128], m[:, 128:]], axis=0).astype(BF)


def spread_kernel(at_ref, own_ref, a1_ref, a2_ref, up_ref, down_ref, o_ref, acc):
    z = at_ref[2]
    sources = [own_ref, a1_ref, a2_ref, up_ref.at[0], up_ref.at[1], up_ref.at[2], down_ref.at[0], down_ref.at[1]]
    for step, source in enumerate(sources):
        to = lax.rem(z + step, Z)
        for layer in range(o_ref.shape[0]):
            o_ref[layer, pl.ds(pl.multiple_of(to * 16, 16), 16), :C] = source[layer, :, :C]
            m = source[layer, :, C:].astype(F32)
            for h in range(2):
                acc[layer, pl.ds(pl.multiple_of(h * 64 + to * 8, 8), 8), :] = m[h * 8 : h * 8 + 8]
    for layer in range(o_ref.shape[0]):
        o_ref[layer, :, C:] = acc[layer].astype(BF)


def flat(refs):
    return [part for ref in refs for part in ([ref] if len(ref.shape) == 2 else [ref.at[i] for i in range(ref.shape[0])])]


def join_kernel(*refs):
    for i, part in enumerate(flat(refs[:-1])):
        refs[-1][i] = part[...]


def build_kernel(at_ref, *refs):
    parts, (w_ref, m_ref, sem) = flat(refs[:-3]), refs[-3:]
    ylo, x, core = at_ref[0], at_ref[1], at_ref[3]
    copies = []
    for i, part in enumerate(parts):
        j, rest = i // 8, i % 8
        c = core if j == 0 else 1 - core
        to = lax.rem(ylo + rest % YLO, YLO) * X + lax.rem(x + rest // YLO, X)
        rows = pl.ds(pl.multiple_of(to * 128, 128), 128)
        copies.append((part.at[:, :C], w_ref.at[rows, pl.ds(pl.multiple_of(c * C, C), C)]))
        rows = pl.ds(pl.multiple_of(to * 64, 64), 64)
        for h in range(2):
            columns = pl.ds(pl.multiple_of(c * 256 + h * 128, 128), 128)
            copies.append((part.at[h * 64 : h * 64 + 64, C:], m_ref.at[rows, columns]))
    copies = [pltpu.make_async_copy(a, b, sem.at[i]) for i, (a, b) in enumerate(copies)]
    for copy in copies:
        copy.start()
    for copy in copies:
        copy.wait()


TILE, BLOCK = 256, 256


def rows_of(delayed, now, w_ref, m_ref):
    both = jnp.concatenate([delayed, now], axis=1)
    gated = []
    for at in range(0, C, BLOCK):
        f = jnp.dot(both, w_ref[:, at : at + BLOCK], preferred_element_type=F32)
        g = jnp.dot(both, w_ref[:, C + at : C + at + BLOCK], preferred_element_type=F32)
        gated.append((jnp.tanh(f) * (0.5 * jnp.tanh(0.5 * g) + 0.5)).astype(BF))
    mix = jnp.dot(jnp.concatenate(gated, axis=1), m_ref[...], preferred_element_type=F32)
    return (now.astype(F32) + mix).astype(BF)


def layer_kernel(count, base, *refs):
    n_d, n_n = count
    ds, ns, (w_ref, m_ref, o_ref), held = refs[:n_d], refs[n_d : n_d + n_n], refs[n_d + n_n : n_d + n_n + 3], refs[n_d + n_n + 3 :]
    whole = []
    for parts in (ds, ns):
        if len(parts) > 1:
            ref, held = held[0], held[1:]
            at = 0
            for part in parts:
                ref[at : at + part.shape[0], :] = part[...]
                at += part.shape[0]
            parts = [ref]
        whole.append(parts[0])
    d_ref, n_ref = whole

    for at in range(0, o_ref.shape[0], TILE):
        count = min(TILE, o_ref.shape[0] - at)
        rows, there = pl.ds(at, count), pl.ds(base + at, count)
        o_ref[rows, :] = rows_of(d_ref[there, :], n_ref[there, :], w_ref, m_ref)


def out_kernel(writes, d_ref, n_ref, *refs):
    count = len(writes)
    befores, (w_ref, m_ref), (o_ref, got_ref, sems) = refs[:count], refs[count : count + 2], refs[-3:]
    sent = [
        pltpu.make_async_copy(before, o_ref.at[layer, at : at + before.shape[0]], sems.at[i])
        for i, (before, (layer, at)) in enumerate(zip(befores, writes))
    ]
    for copy in sent:
        copy.start()
    for at in range(0, d_ref.shape[0], TILE):
        rows = pl.ds(at, min(TILE, d_ref.shape[0] - at))
        got_ref[rows, :] = rows_of(d_ref[rows, :], n_ref[rows, :], w_ref, m_ref)
    for copy in sent:
        copy.wait()


def last_kernel(writes, base, *refs):
    o_ref, got_ref, sems, own_sem = refs[-4:]
    out_kernel(writes, *refs[:-4], o_ref, got_ref, sems)
    copy = pltpu.make_async_copy(got_ref, o_ref.at[1, base : base + got_ref.shape[0]], own_sem)
    copy.start()
    copy.wait()


def cost(rows):
    return pl.CostEstimate(flops=rows * 2 * (4 * C * C + C * C), transcendentals=rows * 2 * C, bytes_accessed=rows * C * 6 + 5 * C * C * 2)


def per_device(signal, kernel_weight_stack, blend_weight_stack):
    layers = kernel_weight_stack.shape[0]
    half = signal.shape[0] // 2
    s, b = lax.axis_index("seq"), lax.axis_index("batch")
    at = jnp.stack([s // (X * Z), s // Z % X, s % Z, b % CORE]).astype(jnp.int32)

    early, late = signal[:half], signal[half:]
    piece = pl.pallas_call(
        pack_kernel,
        out_shape=jax.ShapeDtypeStruct((layers, 16, 640), BF),
        in_specs=[SMEM, VMEM, VMEM],
        out_specs=VMEM,
        compiler_params=params(4),
        name="pack",
    )(at, kernel_weight_stack, blend_weight_stack)

    before_late = [move(late[: half // 2], "seq"), move(late[half // 2 :], "seq")]
    before_early = [move(early, "seq")]
    a1, a2 = move(piece, "z", -1), move(piece, "z", -2)
    down = move(jnp.stack([piece, a1]), "z", 2)
    up = move(jnp.stack([piece, a1, a2]), "z", -3)
    along_z = pl.pallas_call(
        spread_kernel,
        out_shape=jax.ShapeDtypeStruct((layers, 128, 640), BF),
        in_specs=[SMEM] + [VMEM] * 5,
        out_specs=VMEM,
        scratch_shapes=[pltpu.VMEM((layers, 128, 128), F32)],
        compiler_params=params(8),
        name="spread",
    )(at, piece, a1, a2, up, down)

    def join(*parts):
        count = sum(part.size for part in parts) // (128 * 640)
        return pl.pallas_call(
            join_kernel,
            out_shape=jax.ShapeDtypeStruct((count, 128, 640), BF),
            in_specs=[VMEM] * len(parts),
            out_specs=VMEM,
            compiler_params=params(8),
            name="join",
        )(*parts)

    swapped = move(along_z, "y")
    weights = []
    for layer in range(layers):
        own, other = along_z[layer], swapped[layer]
        if layer == 0:
            ahead = move(own, "x", -1)
            along_x = [own, ahead, move(ahead, "x", -1), move(own, "xz")]
            others = [other] + [move(along_x[i], "y") for i in range(1, X)]
            own = [part for pair in zip(along_x, others) for part in pair]
            own += [move(part, "core") for part in own]
        else:
            pairs = [join(own, other)]
            for _ in range(1, X):
                pairs.append(move(pairs[-1], "x", -1))
            own = [join(*pairs)]
            own.append(move(own[0], "core"))
        weights.append(
            pl.pallas_call(
                build_kernel,
                out_shape=(jax.ShapeDtypeStruct((2 * C, 2 * C), BF), jax.ShapeDtypeStruct((C, C), BF)),
                in_specs=[SMEM] + [ANY] * len(own),
                out_specs=(VMEM, VMEM),
                scratch_shapes=[pltpu.SemaphoreType.DMA((48,))],
                compiler_params=params(8),
                name="build",
            )(at, *own)
        )

    def apply(delayed, now, base, rows):
        now = now if isinstance(now, list) else [now]
        held = [pltpu.VMEM((half, C), BF) for parts in (delayed, now) if len(parts) > 1]
        return pl.pallas_call(
            functools.partial(layer_kernel, (len(delayed), len(now)), base),
            out_shape=jax.ShapeDtypeStruct((rows, C), BF),
            in_specs=[VMEM] * (len(delayed) + len(now) + 2),
            out_specs=VMEM,
            scratch_shapes=held,
            compiler_params=params(20),
            cost_estimate=cost(rows),
            name="layer",
        )(*delayed, *now, *weights[0])

    first_early, arriving, base = [], [], 0
    for rows in (half // 8 * 7, half // 8):
        first_early.append(apply(before_late, early, base, rows))
        arriving.append((base, first_early[-1], move(first_early[-1], "seq")))
        base += rows
    first_late = apply([early], late, 0, half)
    before_first_late = apply(before_early, before_late, 0, half)
    out_shape = jax.ShapeDtypeStruct((layers, 2 * half, C), BF)
    rows = lambda n: jax.ShapeDtypeStruct((n, C), BF)
    befores, writes, at = [first_late], [(0, half)], 0
    for part in first_early:
        befores.append(part)
        writes.append((0, at))
        at += part.shape[0]
    steps = [(half, before_first_late, first_late)] + [(base, delayed, now) for base, now, delayed in arriving]
    out = None
    for i, (base, delayed, now) in enumerate(steps):
        count, last = delayed.shape[0], i == len(steps) - 1
        held = [pltpu.VMEM((count, C), BF)] if last else []
        sems = [pltpu.SemaphoreType.DMA((len(befores),))] + [pltpu.SemaphoreType.DMA] * last
        args = [delayed, now, *befores, *weights[1]]
        first = out is None
        got = pl.pallas_call(
            functools.partial(last_kernel, writes, base) if last else functools.partial(out_kernel, writes),
            out_shape=out_shape if last else (out_shape, rows(count)),
            in_specs=[VMEM] * len(args) + ([] if first else [ANY]),
            out_specs=ANY if last else (ANY, VMEM),
            scratch_shapes=held + sems,
            input_output_aliases={} if first else {len(args): 0},
            compiler_params=params(20),
            cost_estimate=cost(count),
            name="second",
        )(*args, *([] if first else [out]))
        out, befores, writes = (got, None, None) if last else (got[0], [got[1]], [(1, base)])
    return out


def solution(mesh):
    return jax.shard_map(
        per_device,
        mesh=mesh,
        in_specs=(P(("batch", "seq"), None), P(None, "seq", None), P(None, "seq", None)),
        out_specs=P(None, ("batch", "seq"), None),
        check_vma=False,
    )
```

```python
import functools

import jax
import jax.numpy as jnp
from jax import lax
from jax.experimental import pallas as pl
from jax.experimental.pallas import tpu as pltpu
from jax.sharding import PartitionSpec as P


AXES = ("seq", "batch")
YLO, X, Z, YHI, CORE = 2, 4, 8, 2, 2
C = 512
BF, F32 = jnp.bfloat16, jnp.float32
VMEM = pl.BlockSpec(memory_space=pltpu.VMEM)
SMEM = pl.BlockSpec(memory_space=pltpu.SMEM)
ANY = pl.BlockSpec(memory_space=pl.ANY)


def place(ylo, x, z, yhi, core):
    return (((ylo * X + x) * Z + z) * YHI + yhi) * CORE + core


def route(kind, step):
    pairs = []
    for ylo in range(YLO):
        for x in range(X):
            for z in range(Z):
                for yhi in range(YHI):
                    for core in range(CORE):
                        to = [ylo, x, z, yhi, core]
                        if kind == "seq":
                            s = (ylo * X + x) * Z + z + step
                            if s >= YLO * X * Z:
                                continue
                            to[:3] = [s // (X * Z), s // Z % X, s % Z]
                        elif kind == "y":
                            y = (yhi * YLO + ylo + (1 if ylo else -1)) % (YHI * YLO)
                            to[0], to[3] = y % YLO, y // YLO
                        elif kind == "x":
                            to[1] = (x + step) % X
                        elif kind == "xz":
                            to[1], to[2] = (x + 1) % X, (z - 1) % Z
                        elif kind == "z":
                            to[2] = (z + step) % Z
                        else:
                            to[4] = 1 - core
                        pairs.append((place(ylo, x, z, yhi, core), place(*to)))
    return pairs


def move(block, kind, step=1):
    return lax.ppermute(block, AXES, route(kind, step))


def params(mib):
    return pltpu.CompilerParams(vmem_limit_bytes=mib << 20)


def pack_kernel(at_ref, k_ref, m_ref, o_ref):
    first = at_ref[3] == 0
    for layer in range(k_ref.shape[0]):
        k = k_ref[layer]
        o_ref[layer, :, :C] = jnp.where(first, k[:, :C], k[:, C:])
        m = m_ref[layer].astype(F32)
        m = jnp.where(first, m[:, :256], m[:, 256:])
        o_ref[layer, :, C:] = jnp.concatenate([m[:, :128], m[:, 128:]], axis=0).astype(BF)


def spread_kernel(at_ref, own_ref, a1_ref, a2_ref, up_ref, down_ref, o_ref, acc):
    z = at_ref[2]
    sources = [own_ref, a1_ref, a2_ref, up_ref.at[0], up_ref.at[1], up_ref.at[2], down_ref.at[0], down_ref.at[1]]
    for step, source in enumerate(sources):
        to = lax.rem(z + step, Z)
        for layer in range(o_ref.shape[0]):
            o_ref[layer, pl.ds(pl.multiple_of(to * 16, 16), 16), :C] = source[layer, :, :C]
            m = source[layer, :, C:].astype(F32)
            for h in range(2):
                acc[layer, pl.ds(pl.multiple_of(h * 64 + to * 8, 8), 8), :] = m[h * 8 : h * 8 + 8]
    for layer in range(o_ref.shape[0]):
        o_ref[layer, :, C:] = acc[layer].astype(BF)


def flat(refs):
    return [part for ref in refs for part in ([ref] if len(ref.shape) == 2 else [ref.at[i] for i in range(ref.shape[0])])]


def join_kernel(*refs):
    for i, part in enumerate(flat(refs[:-1])):
        refs[-1][i] = part[...]


def build_kernel(at_ref, *refs):
    parts, (w_ref, m_ref, sem) = flat(refs[:-3]), refs[-3:]
    ylo, x, core = at_ref[0], at_ref[1], at_ref[3]
    copies = []
    for i, part in enumerate(parts):
        j, rest = i // 8, i % 8
        c = core if j == 0 else 1 - core
        to = lax.rem(ylo + rest % YLO, YLO) * X + lax.rem(x + rest // YLO, X)
        rows = pl.ds(pl.multiple_of(to * 128, 128), 128)
        copies.append((part.at[:, :C], w_ref.at[rows, pl.ds(pl.multiple_of(c * C, C), C)]))
        rows = pl.ds(pl.multiple_of(to * 64, 64), 64)
        for h in range(2):
            columns = pl.ds(pl.multiple_of(c * 256 + h * 128, 128), 128)
            copies.append((part.at[h * 64 : h * 64 + 64, C:], m_ref.at[rows, columns]))
    copies = [pltpu.make_async_copy(a, b, sem.at[i]) for i, (a, b) in enumerate(copies)]
    for copy in copies:
        copy.start()
    for copy in copies:
        copy.wait()


TILE, BLOCK = 256, 256


def rows_of(delayed, now, w_ref, m_ref):
    both = jnp.concatenate([delayed, now], axis=1)
    gated = []
    for at in range(0, C, BLOCK):
        f = jnp.dot(both, w_ref[:, at : at + BLOCK], preferred_element_type=F32)
        g = jnp.dot(both, w_ref[:, C + at : C + at + BLOCK], preferred_element_type=F32)
        gated.append((jnp.tanh(f) * (0.5 * jnp.tanh(0.5 * g) + 0.5)).astype(BF))
    mix = jnp.dot(jnp.concatenate(gated, axis=1), m_ref[...], preferred_element_type=F32)
    return (now.astype(F32) + mix).astype(BF)


def layer_kernel(count, base, *refs):
    n_d, n_n = count
    ds, ns, (w_ref, m_ref, o_ref), held = refs[:n_d], refs[n_d : n_d + n_n], refs[n_d + n_n : n_d + n_n + 3], refs[n_d + n_n + 3 :]
    whole = []
    for parts in (ds, ns):
        if len(parts) > 1:
            ref, held = held[0], held[1:]
            at = 0
            for part in parts:
                ref[at : at + part.shape[0], :] = part[...]
                at += part.shape[0]
            parts = [ref]
        whole.append(parts[0])
    d_ref, n_ref = whole

    for at in range(0, o_ref.shape[0], TILE):
        rows, there = pl.ds(at, TILE), pl.ds(base + at, TILE)
        o_ref[rows, :] = rows_of(d_ref[there, :], n_ref[there, :], w_ref, m_ref)


def out_kernel(writes, d_ref, n_ref, *refs):
    count = len(writes)
    befores, (w_ref, m_ref), (o_ref, got_ref, sems) = refs[:count], refs[count : count + 2], refs[-3:]
    sent = [
        pltpu.make_async_copy(before, o_ref.at[layer, at : at + before.shape[0]], sems.at[i])
        for i, (before, (layer, at)) in enumerate(zip(befores, writes))
    ]
    for copy in sent:
        copy.start()
    for at in range(0, d_ref.shape[0], TILE):
        rows = pl.ds(at, TILE)
        got_ref[rows, :] = rows_of(d_ref[rows, :], n_ref[rows, :], w_ref, m_ref)
    for copy in sent:
        copy.wait()


def last_kernel(writes, base, *refs):
    o_ref, got_ref, sems, own_sem = refs[-4:]
    out_kernel(writes, *refs[:-4], o_ref, got_ref, sems)
    copy = pltpu.make_async_copy(got_ref, o_ref.at[1, base : base + got_ref.shape[0]], own_sem)
    copy.start()
    copy.wait()


def cost(rows):
    return pl.CostEstimate(flops=rows * 2 * (4 * C * C + C * C), transcendentals=rows * 2 * C, bytes_accessed=rows * C * 6 + 5 * C * C * 2)


def per_device(signal, kernel_weight_stack, blend_weight_stack):
    layers = kernel_weight_stack.shape[0]
    half = signal.shape[0] // 2
    s, b = lax.axis_index("seq"), lax.axis_index("batch")
    at = jnp.stack([s // (X * Z), s // Z % X, s % Z, b % CORE]).astype(jnp.int32)

    early, late = signal[:half], signal[half:]
    piece = pl.pallas_call(
        pack_kernel,
        out_shape=jax.ShapeDtypeStruct((layers, 16, 640), BF),
        in_specs=[SMEM, VMEM, VMEM],
        out_specs=VMEM,
        compiler_params=params(4),
        name="pack",
    )(at, kernel_weight_stack, blend_weight_stack)

    before_late = [move(late[: half // 2], "seq"), move(late[half // 2 :], "seq")]
    before_early = [move(early, "seq")]
    a1, a2 = move(piece, "z", -1), move(piece, "z", -2)
    down = move(jnp.stack([piece, a1]), "z", 2)
    up = move(jnp.stack([piece, a1, a2]), "z", -3)
    along_z = pl.pallas_call(
        spread_kernel,
        out_shape=jax.ShapeDtypeStruct((layers, 128, 640), BF),
        in_specs=[SMEM] + [VMEM] * 5,
        out_specs=VMEM,
        scratch_shapes=[pltpu.VMEM((layers, 128, 128), F32)],
        compiler_params=params(8),
        name="spread",
    )(at, piece, a1, a2, up, down)

    def join(*parts):
        count = sum(part.size for part in parts) // (128 * 640)
        return pl.pallas_call(
            join_kernel,
            out_shape=jax.ShapeDtypeStruct((count, 128, 640), BF),
            in_specs=[VMEM] * len(parts),
            out_specs=VMEM,
            compiler_params=params(8),
            name="join",
        )(*parts)

    swapped = move(along_z, "y")
    weights = []
    for layer in range(layers):
        own, other = along_z[layer], swapped[layer]
        if layer == 0:
            ahead = move(own, "x", -1)
            along_x = [own, ahead, move(ahead, "x", -1), move(own, "xz")]
            others = [other] + [move(along_x[i], "y") for i in range(1, X)]
            own = [part for pair in zip(along_x, others) for part in pair]
            own += [move(part, "core") for part in own]
        else:
            pairs = [join(own, other)]
            for _ in range(1, X):
                pairs.append(move(pairs[-1], "x", -1))
            own = [join(*pairs)]
            own.append(move(own[0], "core"))
        weights.append(
            pl.pallas_call(
                build_kernel,
                out_shape=(jax.ShapeDtypeStruct((2 * C, 2 * C), BF), jax.ShapeDtypeStruct((C, C), BF)),
                in_specs=[SMEM] + [ANY] * len(own),
                out_specs=(VMEM, VMEM),
                scratch_shapes=[pltpu.SemaphoreType.DMA((48,))],
                compiler_params=params(8),
                name="build",
            )(at, *own)
        )

    def apply(delayed, now, base, rows):
        now = now if isinstance(now, list) else [now]
        held = [pltpu.VMEM((half, C), BF) for parts in (delayed, now) if len(parts) > 1]
        return pl.pallas_call(
            functools.partial(layer_kernel, (len(delayed), len(now)), base),
            out_shape=jax.ShapeDtypeStruct((rows, C), BF),
            in_specs=[VMEM] * (len(delayed) + len(now) + 2),
            out_specs=VMEM,
            scratch_shapes=held,
            compiler_params=params(20),
            cost_estimate=cost(rows),
            name="layer",
        )(*delayed, *now, *weights[0])

    first_early, arriving, base = [], [], 0
    for rows in (half // 2, half // 4, half // 4):
        first_early.append(apply(before_late, early, base, rows))
        arriving.append((base, first_early[-1], move(first_early[-1], "seq")))
        base += rows
    first_late = apply([early], late, 0, half)
    before_first_late = apply(before_early, before_late, 0, half)
    out_shape = jax.ShapeDtypeStruct((layers, 2 * half, C), BF)
    rows = lambda n: jax.ShapeDtypeStruct((n, C), BF)
    befores, writes, at = [first_late], [(0, half)], 0
    for part in first_early:
        befores.append(part)
        writes.append((0, at))
        at += part.shape[0]
    steps = [(half, before_first_late, first_late)] + [(base, delayed, now) for base, now, delayed in arriving]
    out = None
    for i, (base, delayed, now) in enumerate(steps):
        count, last = delayed.shape[0], i == len(steps) - 1
        held = [pltpu.VMEM((count, C), BF)] if last else []
        sems = [pltpu.SemaphoreType.DMA((len(befores),))] + [pltpu.SemaphoreType.DMA] * last
        args = [delayed, now, *befores, *weights[1]]
        first = out is None
        got = pl.pallas_call(
            functools.partial(last_kernel, writes, base) if last else functools.partial(out_kernel, writes),
            out_shape=out_shape if last else (out_shape, rows(count)),
            in_specs=[VMEM] * len(args) + ([] if first else [ANY]),
            out_specs=ANY if last else (ANY, VMEM),
            scratch_shapes=held + sems,
            input_output_aliases={} if first else {len(args): 0},
            compiler_params=params(20),
            cost_estimate=cost(count),
            name="second",
        )(*args, *([] if first else [out]))
        out, befores, writes = (got, None, None) if last else (got[0], [got[1]], [(1, base)])
    return out


def solution(mesh):
    return jax.shard_map(
        per_device,
        mesh=mesh,
        in_specs=(P(("batch", "seq"), None), P(None, "seq", None), P(None, "seq", None)),
        out_specs=P(None, ("batch", "seq"), None),
        check_vma=False,
    )
```
